32 devices in a mesh: gx: 4 (over z), gy: 2 (over x), gz: 4 (over y, core).
Axes of the slice: x: 2, y: 2, z: 4, core: 2. Of those that a mesh axis runs over, the one named last changes fastest.
Arguments:
- coords: float32 [3, 4, 2, 4, 2048], P(None, 'gx', 'gy', 'gz'), may hold values from 0 to 6
- charges: float32 [2, 4, 2, 4, 2048], P(None, 'gx', 'gy', 'gz'), may hold values from -8 to 8
- dipoles: float32 [6, 4, 2, 4, 2048], P(None, 'gx', 'gy', 'gz'), may hold values from -6 to 6
- polar: float32 [2, 4, 2, 4, 2048], P(None, 'gx', 'gy', 'gz'), may hold values from 0.08 to 0.25
- perturbed: int32 [4, 2, 4, 2048], P('gx', 'gy', 'gz'), may hold values 0 or 1
- cluster_order: int32 [4, 2, 4, 2048], P('gx', 'gy', 'gz'), may hold values from 0 to 2047, each once within a row
- border_clusters: int32 [4, 2, 4, 4], P('gx', 'gy', 'gz'), may hold values from 0 to 15, as said below
- tile_list: int32 [3, 4, 2, 4, 128], P(None, 'gx', 'gy', 'gz'), may hold values from 0 to 26, as said below
- tile_count: int32 [4, 2, 4], P('gx', 'gy', 'gz'), may hold values from 112 to 128, as said below
Outputs:
- induced: float32 [6, 4, 2, 4, 2048], P(None, 'gx', 'gy', 'gz')
The draws below stay inside these ranges and needn't reach their ends.
Inputs may be any that keep to these rules, and one draw needn't show every extreme that they name: `border_clusters`: each brick's entries are distinct cluster numbers of that brick. `tile_list`: row 0 is a cluster of the brick itself (0 to 15); row 1 a neighbour slot (0 to 26, 13 is the brick itself); row 2 is a cluster of the brick itself (0 to 15) where row 1 is 13, else a position (0 to 3) in the neighbour's border_clusters. Among the first 104 tiles of each brick, every pair of a neighbour slot other than 13 and a border position appears exactly once. `tile_count`: some brick uses all 128 tiles in every draw.
All inputs are finite; a program needn't handle non-finite values. No bound on the sum of `perturbed` on one device may be relied on, other than what follows from the above.
Results may differ from the reference program's by a relative error of at most 0.0003.
Values sent between devices are 32-bit elements; how exact they have to be, the bound alone decides.
No kernel may reach another device: no remote copies, remote signals or barrier semaphores. Data moves between devices by JAX's collectives and lax.ppermute only.
A program may use at most 64 MiB of HBM per device.

```python
import math
import jax
import jax.numpy as jnp
from jax import lax

CLU_DEV = 16
ITERS = 3
ATOM_DEV = 2048
BORDER_CLU = 4
TILE_DEV = 128
N_GX = 4
N_GY = 2
N_GZ = 4


def draw_border_clusters(key, part):
    scores = jax.random.randint(jax.random.fold_in(key, 301), (N_GX, N_GY, N_GZ, CLU_DEV), 0, 1 << 20)
    scores = scores * CLU_DEV + jnp.arange(CLU_DEV, dtype=jnp.int32)
    ranking = jnp.argsort(scores, axis=-1)
    return ranking[..., :BORDER_CLU].astype(jnp.int32)


def draw_tile_list(key, part):
    subkeys = jax.random.split(jax.random.fold_in(key, 302), 6)
    grid_shape = (N_GX, N_GY, N_GZ, TILE_DEV)
    covering = 26 * BORDER_CLU
    position = jnp.arange(TILE_DEV, dtype=jnp.int32)
    recv_id = jax.random.randint(subkeys[0], grid_shape, 0, CLU_DEV)
    own_brick = jax.random.randint(subkeys[1], grid_shape, 0, 2) == 0
    random_slot = jnp.where(own_brick, 13, jax.random.randint(subkeys[2], grid_shape, 0, 27))
    own_source = jax.random.randint(subkeys[3], grid_shape, 0, CLU_DEV)
    far_source = jax.random.randint(subkeys[4], grid_shape, 0, BORDER_CLU)
    random_source = jnp.where(random_slot == 13, own_source, far_source)
    scores = jax.random.randint(subkeys[5], grid_shape, 0, 1 << 18) * TILE_DEV + position
    scores = jnp.where(position < covering, scores, (1 << 18) * TILE_DEV + position)
    ordering = jnp.argsort(scores, axis=-1).astype(jnp.int32)
    direction = ordering // BORDER_CLU
    cover_slot = direction + (direction >= 13).astype(jnp.int32)
    cover_source = ordering % BORDER_CLU
    in_cover = position < covering
    slot_id = jnp.where(in_cover, cover_slot, random_slot)
    source = jnp.where(in_cover, cover_source, random_source)
    return jnp.stack([recv_id, slot_id, source]).astype(jnp.int32)


def draw_tile_count(key, part):
    subkeys = jax.random.split(jax.random.fold_in(key, 303), 2)
    bricks = N_GX * N_GY * N_GZ
    totals = TILE_DEV - jax.random.randint(subkeys[0], (bricks,), 0, TILE_DEV // 8 + 1)
    fullest = jax.random.randint(subkeys[1], (), 0, bricks)
    totals = totals.at[fullest].set(TILE_DEV)
    return totals.reshape(N_GX, N_GY, N_GZ).astype(jnp.int32)


def plant(array, key, low, largest):
    dims = array.shape
    index_at = [jax.random.randint(jax.random.fold_in(key, axis), (), 0, dims[axis]) for axis in range(len(dims))]
    array = array.at[tuple(index_at)].set(low)
    longest = dims.index(max(dims))
    index_at[longest] = (index_at[longest] + 1) % dims[longest]
    return array.at[tuple(index_at)].set(largest)


def levels(own_key, dims, cuts, least, high):
    loudness, own = 1.0, jax.random.fold_in(own_key, 6)
    for axis_at, shards_of in cuts:
        steps = jnp.exp(jax.random.uniform(jax.random.fold_in(own, axis_at), (shards_of,), jnp.float32, least / len(cuts), high / len(cuts)))
        loudness = loudness * jnp.repeat(steps, dims[axis_at] // shards_of).reshape([-1 if axis == axis_at else 1 for axis in range(len(dims))])
    return loudness


def bell_draw(key, extent, scale, most, cuts=(), kind=jnp.bfloat16):
    loudness = levels(key, extent, cuts, -0.22, 0.18) if cuts else 1.0
    drawn = jax.random.normal(key, extent, jnp.float32) * scale * loudness
    return jnp.minimum(jnp.maximum(drawn, -most), most).astype(kind)


def setup_inputs(seed: int = 0) -> dict:
    splits = jax.random.split(jax.random.key(seed), 10)
    return {
        "coords": jnp.clip(6.0 * jax.random.uniform(splits[0], (3, N_GX, N_GY, N_GZ, ATOM_DEV), jnp.float32) ** levels(splits[0], (3, N_GX, N_GY, N_GZ, ATOM_DEV), ((1, 4), (2, 2), (3, 4)), -0.2, 0.2), 0.0, 6.0),
        "charges": bell_draw(splits[1], (2, N_GX, N_GY, N_GZ, ATOM_DEV), 2.0, 8.0, ((1, 4), (2, 2), (3, 4)), jnp.float32),
        "dipoles": bell_draw(splits[2], (6, N_GX, N_GY, N_GZ, ATOM_DEV), 1.0, 6.0, ((1, 4), (2, 2), (3, 4)), jnp.float32),
        "polar": jnp.clip(jnp.exp(math.log(0.25) - 1.1394343 * jax.random.uniform(splits[3], (2, N_GX, N_GY, N_GZ, ATOM_DEV), jnp.float32) ** levels(splits[3], (2, N_GX, N_GY, N_GZ, ATOM_DEV), ((1, 4), (2, 2), (3, 4)), -0.2, 0.2)), 0.08, 0.25),
        "perturbed": plant((jax.random.randint(splits[4], (N_GX, N_GY, N_GZ, ATOM_DEV), 0, 4) < 1).astype(jnp.int32), jax.random.fold_in(splits[4], 1), 0, 1),
        "cluster_order": jax.vmap(lambda own: jax.random.permutation(own, ATOM_DEV))(jax.random.split(splits[5], N_GX * N_GY * N_GZ)).reshape((N_GX, N_GY, N_GZ, ATOM_DEV)).astype(jnp.int32),
        "border_clusters": draw_border_clusters(jax.random.fold_in(splits[9], 71), 0),
        "tile_list": draw_tile_list(jax.random.fold_in(splits[9], 71), 0),
        "tile_count": draw_tile_count(jax.random.fold_in(splits[9], 71), 0),
    }


brick_len = 6.0
damping = 1.0
tile_block = 8

def tile_fields(recv_places, source_places, source_data, tile_rows, tile_total, charged):
    clusters = recv_places.shape[1]
    border = (source_places.shape[1] - clusters) // 27
    tile_num = tile_rows.shape[1]
    blocks = tile_num // tile_block
    recv_id = tile_rows[0]
    slot_id = tile_rows[1]
    source = tile_rows[2]
    source_row = jnp.where(slot_id == 13, source, clusters + slot_id * border + source).astype(jnp.int32)
    shifts = jnp.stack([slot_id // 9 - 1, slot_id // 3 % 3 - 1, slot_id % 3 - 1], axis=1).astype(jnp.float32) * brick_len
    usable = (jnp.arange(tile_num, dtype=jnp.int32) < tile_total).astype(jnp.float32)
    same_tile = ((slot_id == 13) & (recv_id == source)).astype(jnp.float32)
    identity = jnp.eye(128, dtype=jnp.float32)

    def one_block(block_args):
        block_recv, block_row, block_shift, block_use, block_same = block_args
        recv_xyz = jnp.take(recv_places, block_recv, axis=1)
        source_xyz = jnp.take(source_places, block_row, axis=1) + block_shift.T[:, :, None]
        values = jnp.take(source_data, block_row, axis=1)
        separation = recv_xyz[:, :, :, None] - source_xyz[:, :, None, :]
        squared = lax.optimization_barrier(jnp.sum(separation * separation, axis=0)) + damping
        inverse = lax.rsqrt(squared)
        weight_mask = block_use[:, None, None] * (1.0 - block_same[:, None, None] * identity)
        third_power = inverse * inverse * inverse * weight_mask
        fifth_power = third_power * inverse * inverse
        pieces = []
        for which_state in range(2):
            first_row = 2 + 3 * which_state if charged else 3 * which_state
            moment = values[first_row:first_row + 3][:, :, None, :]
            projection = lax.optimization_barrier(jnp.sum(moment * separation, axis=0))
            radial = 3.0 * projection * fifth_power
            if charged:
                radial = radial + values[which_state][:, None, :] * third_power
            pieces.append(lax.optimization_barrier(jnp.sum(radial[None] * separation - moment * third_power[None], axis=3)))
        return jnp.concatenate(pieces, axis=0)
    shaped = (recv_id.reshape(blocks, tile_block), source_row.reshape(blocks, tile_block), shifts.reshape(blocks, tile_block, 3), usable.reshape(blocks, tile_block), same_tile.reshape(blocks, tile_block))
    block_sums = lax.map(one_block, shaped)
    block_sums = jnp.transpose(block_sums, (0, 2, 1, 3)).reshape(tile_num, 6 * 128)
    member = (recv_id[:, None] == jnp.arange(clusters, dtype=jnp.int32)[None, :]).astype(jnp.float32)
    summed = jnp.dot(member.T, block_sums, precision=lax.Precision.HIGHEST)
    return jnp.transpose(summed.reshape(clusters, 6, 128), (1, 0, 2))

def reference(coords, charges, dipoles, polar, perturbed, cluster_order, border_clusters, tile_list, tile_count):
    grid = coords.shape[1:4]
    atoms = coords.shape[4]
    clusters = atoms // 128
    border = border_clusters.shape[-1]
    devices_all = grid[0] * grid[1] * grid[2]
    changed = perturbed[None] == 1
    charge_both = jnp.concatenate([charges[:1], jnp.where(changed, charges[1:], charges[:1])], 0)
    moments = jnp.concatenate([dipoles[:3], jnp.where(changed, dipoles[3:], dipoles[:3])], 0)
    polar_both = jnp.concatenate([polar[:1], jnp.where(changed, polar[1:], polar[:1])], 0)

    def arrange(vector):
        return jnp.take_along_axis(vector, jnp.broadcast_to(cluster_order[None], vector.shape), axis=-1)
    places = arrange(coords)
    multipoles = arrange(jnp.concatenate([charge_both, moments], 0))
    response = arrange(jnp.repeat(polar_both, 3, axis=0))
    border_atoms = (border_clusters[..., :, None] * 128 + jnp.arange(128, dtype=jnp.int32)).reshape(grid + (border * 128,)).astype(jnp.int32)

    def neighbourhood(vector):
        rows_count = vector.shape[0]
        chosen = jnp.take_along_axis(vector, jnp.broadcast_to(border_atoms[None], (rows_count,) + border_atoms.shape), axis=-1)
        rolled = [jnp.roll(chosen, (-ox, -oy, -oz), axis=(1, 2, 3)) for ox in (-1, 0, 1) for oy in (-1, 0, 1) for oz in (-1, 0, 1)]
        stacked = jnp.stack(rolled, 1).reshape(rows_count, 27, devices_all, border, 128)
        return jnp.moveaxis(stacked, 2, 1).reshape(rows_count, devices_all, 27 * border, 128)

    def local_blocks(vector):
        return vector.reshape(vector.shape[0], devices_all, clusters, 128)
    recv_blocks = local_blocks(places)
    place_source = jnp.concatenate([recv_blocks, neighbourhood(places)], 2)
    tiles_flat = tile_list.reshape(3, devices_all, -1)
    totals = tile_count.reshape(devices_all)

    def fields(vector, charged):
        source_data = jnp.concatenate([local_blocks(vector), neighbourhood(vector)], 2)

        def per_device(device_args):
            recv_one, place_one, data_one, tile_one, total_one = device_args
            return tile_fields(recv_one, place_one, data_one, tile_one, total_one, charged)
        device_fields = lax.map(per_device, (jnp.moveaxis(recv_blocks, 1, 0), jnp.moveaxis(place_source, 1, 0), jnp.moveaxis(source_data, 1, 0), jnp.moveaxis(tiles_flat, 1, 0), totals))
        return jnp.moveaxis(device_fields, 0, 1).reshape((6,) + grid + (atoms,))

    def state_sums(vector):
        return lax.optimization_barrier(jnp.sum(vector.reshape(2, -1), axis=1))

    def spread(values):
        return jnp.repeat(values, 3)[:, None, None, None, None]
    permanent = fields(multipoles, True)
    induced = response * permanent
    residual = fields(induced, False)
    scaled = response * residual
    direction = scaled
    norm_now = state_sums(residual * scaled)
    for sweep in range(ITERS):
        image = direction / response - fields(direction, False)
        step_len = norm_now / state_sums(direction * image)
        induced = induced + spread(step_len) * direction
        residual = residual - spread(step_len) * image
        if sweep + 1 < ITERS:
            scaled = response * residual
            norm_next = state_sums(residual * scaled)
            direction = scaled + spread(norm_next / norm_now) * direction
            norm_now = norm_next
    inverse_order = jnp.argsort(cluster_order, axis=-1).astype(jnp.int32)
    return jnp.take_along_axis(induced, jnp.broadcast_to(inverse_order[None], induced.shape), axis=-1)
```

```python
import jax
import jax.numpy as jnp
from jax import lax
from jax.experimental import pallas as pl
from jax.experimental.pallas import tpu as pltpu
from jax.sharding import PartitionSpec as P

ITERS = 3
LANES = 128
BRICK = 6.0
STATES = 2
COLS = 16
QCOLS = 4
F32 = jnp.float32
BF16 = jnp.bfloat16
AXES = ("gx", "gy", "gz")
GRAM = tuple((a, b) for a in range(ITERS) for b in range(a, ITERS + 1))

VMEM = pl.BlockSpec(memory_space=pltpu.VMEM)
SMEM = pl.BlockSpec(memory_space=pltpu.SMEM)


def thirds(value):
    high = value.astype(BF16).astype(F32)
    rest = value - high
    middle = rest.astype(BF16).astype(F32)
    return high, middle, rest - middle


def call(kernel, shapes, spaces, scratch=(), limit=None):
    return pl.pallas_call(
        kernel,
        out_shape=[jax.ShapeDtypeStruct(shape, dtype) for shape, dtype in shapes],
        in_specs=spaces,
        out_specs=[VMEM] * len(shapes),
        scratch_shapes=list(scratch),
        compiler_params=pltpu.CompilerParams(vmem_limit_bytes=limit),
    )


def lane_take(rows, lane):
    return jnp.take_along_axis(rows, lane, axis=1, mode="promise_in_bounds")


def permuted(order, rows):
    chunks = order.shape[0]
    lane, chunk = order & (LANES - 1), order >> 7
    picked = [jnp.zeros(order.shape, F32) for _ in rows]
    for c in range(chunks):
        here = chunk == c
        for k, row in enumerate(rows):
            taken = lane_take(jnp.broadcast_to(row[c : c + 1, :], order.shape), lane)
            picked[k] = jnp.where(here, taken, picked[k])
    return picked


def prepare_kernel(coords, charges, dipoles, polar, perturbed, order, border,
                   place, multi, response, outgoing):
    changed = perturbed[...] == 1
    rows = [coords[k] - 0.5 * BRICK for k in range(3)]
    rows += [charges[0], jnp.where(changed, charges[1], charges[0])]
    rows += [dipoles[k] for k in range(3)]
    rows += [jnp.where(changed, dipoles[3 + k], dipoles[k]) for k in range(3)]
    rows += [polar[0], jnp.where(changed, polar[1], polar[0])]
    done = permuted(order[...], rows)
    for k in range(3):
        place[k] = done[k]
    for k in range(8):
        multi[k] = done[3 + k]
    for k in range(2):
        response[k] = done[11 + k]
    for b in range(outgoing.shape[1]):
        row = pl.ds(border[b], 1)
        for k in range(3):
            outgoing[k, pl.ds(b, 1), :] = place[k, row, :]
        for k in range(8):
            outgoing[3 + k, pl.ds(b, 1), :] = multi[k, row, :]


def inverse_kernel(order, inverse):
    clusters = order.shape[0]
    column = jnp.transpose(order[...].astype(F32))
    lanes = lax.broadcasted_iota(jnp.int32, (8, LANES), 1).astype(F32)
    subs = lax.broadcasted_iota(jnp.int32, (8, LANES), 0).astype(F32)
    total = [jnp.zeros((8, LANES), F32) for _ in range(clusters)]
    for c in range(clusters):
        for g in range(LANES // 8):
            value = jnp.broadcast_to(column[8 * g : 8 * g + 8, c : c + 1], (8, LANES))
            slot = subs + float(c * LANES + 8 * g)
            for a in range(clusters):
                total[a] = jnp.where(value == lanes + float(a * LANES), slot, total[a])
    for a in range(clusters):
        inverse[a : a + 1, :] = jnp.sum(total[a], axis=0, keepdims=True).astype(jnp.int32)


def tile_row(tiles, count, clusters, border, t):
    slot = tiles[1, t]
    source = tiles[2, t]
    row = jnp.where(slot == 13, source, clusters + slot * border + source)
    return jnp.where(t < count[0], row, clusters + 13 * border)


def gather_rows(target, own, halo, where, border, shift=False):
    clusters = own.shape[1]
    kinds = own.shape[0]
    for k in range(kinds):
        target[k, 0:clusters, :] = own[k]
    for slot in range(27):
        base = clusters + slot * border
        for k in range(kinds):
            if slot == 13:
                piece = jnp.zeros((border, LANES), F32)
            else:
                ref, index = where[slot]
                piece = halo[ref][index + (k + (0 if shift else 0),)]
            target[k, base : base + border, :] = piece
    used = clusters + 27 * border
    for k in range(kinds):
        if target.shape[1] > used:
            target[k, used:, :] = jnp.zeros((target.shape[1] - used, LANES), F32)


def write_columns(flat, y, v, rows):
    width = STATES * COLS
    for g in range(rows // 8):
        at = slice(8 * g, 8 * g + 8)
        ys = [y[k, at, :] for k in range(3)]
        far = ys[0] * ys[0] + ys[1] * ys[1] + ys[2] * ys[2]
        for s in range(STATES):
            vs = [v[3 * s + k, at, :] for k in range(3)]
            out = list(vs)
            prods = [[vs[b] * ys[k] for k in range(3)] for b in range(3)]
            for b in range(3):
                out += prods[b]
            trace = 3.0 * (prods[0][0] + prods[1][1] + prods[2][2])
            out += [trace * ys[b] - far * vs[b] for b in range(3)]
            out.append(jnp.zeros((8, LANES), F32))
            for c in range(COLS):
                flat[pl.ds(8 * g * width + s * COLS + c, 8, stride=width), :] = out[c]


def split_columns(flat, parts, rows):
    width = STATES * COLS

    def one(r, carry):
        block = flat[pl.ds(pl.multiple_of(r * width, 8), width), :]
        parts[r] = jnp.concatenate(thirds(block), axis=0).astype(BF16)
        return carry

    lax.fori_loop(0, rows, one, None, unroll=4)


def fold(product):
    width = STATES * COLS
    return product[0:width] + product[width : 2 * width] + product[2 * width : 3 * width]


def combine(sums, x, v, selves):
    clusters = x[0].shape[0]
    width = STATES * COLS
    reach = x[0] * x[0] + x[1] * x[1] + x[2] * x[2] + 1.0
    fields = []
    for s in range(STATES):
        def col(c):
            return sums[pl.ds(s * COLS + c, clusters, stride=width), :]

        plain = [col(b) for b in range(3)]
        cross = [[col(3 + 3 * b + k) for k in range(3)] for b in range(3)]
        outer = [col(12 + b) for b in range(3)]
        inner = x[0] * plain[0] + x[1] * plain[1] + x[2] * plain[2]
        inner = 3.0 * (inner - (cross[0][0] + cross[1][1] + cross[2][2]))
        for b in range(3):
            value = x[b] * inner - reach * plain[b] + outer[b]
            for k in range(3):
                value = value + x[k] * (2.0 * cross[b][k] - 3.0 * cross[k][b])
            fields.append(value + selves * v[3 * s + b])
    return fields


def build_kernel(where, parts_of, *refs):
    tiles, count, border_ids, place, multi, response = refs[:6]
    halo = refs[6 : 6 + parts_of]
    induced, outgoing, matrix, y, selves = refs[6 + parts_of : 11 + parts_of]
    sources, flat, flat_q, parts, parts_q, turned, sums, sums_q = refs[11 + parts_of :]
    clusters = place.shape[1]
    border = outgoing.shape[1]
    padded = y.shape[1]
    tile_num = tiles.shape[1]
    qwidth = STATES * QCOLS

    for k in range(3):
        y[k, 0:clusters, :] = place[k]
        y[k, clusters:, :] = jnp.zeros((padded - clusters, LANES), F32)
    for k in range(8):
        sources[k, 0:clusters, :] = multi[k]
        sources[k, clusters:, :] = jnp.zeros((padded - clusters, LANES), F32)
    for slot in range(27):
        if slot == 13:
            continue
        ref, index = where[slot]
        base = clusters + slot * border
        offset = (slot // 9 - 1, slot // 3 % 3 - 1, slot % 3 - 1)
        for k in range(3):
            y[k, base : base + border, :] = halo[ref][index + (k,)] + BRICK * offset[k]
        for k in range(8):
            sources[k, base : base + border, :] = halo[ref][index + (3 + k,)]
    for k in range(3):
        turned[k] = jnp.transpose(y[k])

    write_columns(flat, y, sources.at[pl.ds(2, 6)], padded)
    for g in range(padded // 8):
        at = slice(8 * g, 8 * g + 8)
        for s in range(STATES):
            charge = sources[s, at, :]
            out = [charge] + [charge * y[k, at, :] for k in range(3)]
            for c in range(QCOLS):
                flat_q[pl.ds(8 * g * qwidth + s * QCOLS + c, 8, stride=qwidth), :] = out[c]
    split_columns(flat, parts, padded)

    def one_q(r, carry):
        block = flat_q[pl.ds(pl.multiple_of(r * qwidth, 8), qwidth), :]
        pieces = thirds(block) + (jnp.zeros_like(block),)
        parts_q[r] = jnp.concatenate(pieces, axis=0).astype(BF16)
        return carry

    lax.fori_loop(0, padded, one_q, None, unroll=4)

    sums[...] = jnp.zeros_like(sums)
    sums_q[...] = jnp.zeros_like(sums_q)
    selves[...] = jnp.zeros_like(selves)
    width = STATES * COLS

    def one(t, carry):
        recv = tiles[0, t]
        row = tile_row(tiles, count, clusters, border, t)
        same = jnp.logical_and(row == recv, row < clusters)
        pick = jnp.full((LANES, LANES), row, jnp.int32)
        d = [
            place[k, pl.ds(recv, 1), :] - lane_take(turned[k], pick)
            for k in range(3)
        ]
        squared = d[0] * d[0] + (d[1] * d[1] + (d[2] * d[2] + 1.0))
        inverse = lax.rsqrt(squared)
        second = inverse * inverse
        g3 = second * inverse
        g5 = g3 * second
        high = g5.astype(BF16)
        low = (g5 - high.astype(F32)).astype(BF16)
        matrix[t, 0:LANES, :] = high
        matrix[t, LANES:, :] = low
        left = parts[row]
        both = jnp.concatenate([high, low], axis=0)
        product = jnp.dot(jnp.concatenate([left, left], axis=1), both, preferred_element_type=F32)
        at = pl.ds(pl.multiple_of(recv * width, 8), width)
        sums[at, :] += fold(product)
        high = g3.astype(BF16)
        low = (g3 - high.astype(F32)).astype(BF16)
        left = parts_q[row]
        both = jnp.concatenate([high, low], axis=0)
        product = jnp.dot(jnp.concatenate([left, left], axis=1), both, preferred_element_type=F32)
        at = pl.ds(pl.multiple_of(recv * qwidth, 8), qwidth)
        sums_q[at, :] += product[0:qwidth] + product[qwidth : 2 * qwidth] + product[2 * qwidth : 3 * qwidth]
        at = pl.ds(recv, 1)
        selves[at, :] += jnp.where(same, 1.0, 0.0).astype(F32)
        return carry

    lax.fori_loop(0, tile_num, one, None, unroll=2)

    x = [place[k] for k in range(3)]
    fields = combine(sums, x, [multi[2 + k] for k in range(6)], selves[...])
    for s in range(STATES):
        def col(c):
            return sums_q[pl.ds(s * QCOLS + c, clusters, stride=qwidth), :]

        whole = col(0)
        for b in range(3):
            value = fields[3 * s + b] + (x[b] * whole - col(1 + b))
            induced[3 * s + b] = response[s] * value
    send_border(induced, outgoing, border_ids)


def send_border(vector, outgoing, border_ids):
    for b in range(outgoing.shape[1]):
        row = pl.ds(border_ids[b], 1)
        for k in range(vector.shape[0]):
            outgoing[k, pl.ds(b, 1), :] = vector[k, row, :]


def field_of(where, tiles, count, y, selves, matrix, own, halo, scratch, border):
    sources, flat, parts, sums = scratch
    clusters = own.shape[1]
    padded = y.shape[1]
    width = STATES * COLS
    for k in range(6):
        sources[k, 0:clusters, :] = own[k]
        sources[k, clusters:, :] = jnp.zeros((padded - clusters, LANES), F32)
    for slot in range(27):
        if slot == 13:
            continue
        ref, index = where[slot]
        base = clusters + slot * border
        for k in range(6):
            sources[k, base : base + border, :] = halo[ref][index + (k,)]
    write_columns(flat, y, sources, padded)
    split_columns(flat, parts, padded)
    sums[...] = jnp.zeros_like(sums)

    def one(t, carry):
        recv = tiles[0, t]
        row = tile_row(tiles, count, clusters, border, t)
        left = parts[row]
        product = jnp.dot(
            jnp.concatenate([left, left], axis=1), matrix[t], preferred_element_type=F32
        )
        at = pl.ds(pl.multiple_of(recv * width, 8), width)
        sums[at, :] += fold(product)
        return carry

    lax.fori_loop(0, tiles.shape[1], one, None, unroll=4)
    x = [y[k, 0:clusters, :] for k in range(3)]
    return combine(sums, x, [own[k] for k in range(6)], selves[...])


def step_kernel(where, parts_of, *refs):
    tiles, count, border_ids, response, y, selves, matrix, own = refs[:8]
    halo = refs[8 : 8 + parts_of]
    plain, scaled, outgoing = refs[8 + parts_of : 11 + parts_of]
    scratch = refs[11 + parts_of :]
    border = outgoing.shape[1]
    fields = field_of(where, tiles, count, y, selves, matrix, own, halo, scratch, border)
    for k in range(6):
        plain[k] = fields[k]
        scaled[k] = response[k // 3] * fields[k]
    send_border(scaled, outgoing, border_ids)


def last_kernel(where, parts_of, border, *refs):
    tiles, count, response, y, selves, matrix = refs[:6]
    plains = refs[6 : 6 + ITERS]
    scaleds = refs[6 + ITERS : 6 + 2 * ITERS]
    base = 6 + 2 * ITERS
    halo = refs[base : base + parts_of]
    gram = refs[base + parts_of]
    scratch = refs[base + parts_of + 1 :]
    own = scaleds[-1]
    fields = field_of(where, tiles, count, y, selves, matrix, own, halo, scratch, border)
    lane = lax.broadcasted_iota(jnp.int32, (1, LANES), 1)
    total = jnp.zeros((1, LANES), F32)
    for s in range(STATES):
        for e, (a, b) in enumerate(GRAM):
            sum_of = None
            for k in range(3 * s, 3 * s + 3):
                right = scaleds[b][k] if b < ITERS else response[s] * fields[k]
                term = plains[a][k] * right
                sum_of = term if sum_of is None else sum_of + term
            value = jnp.sum(jnp.sum(sum_of, axis=0, keepdims=True), axis=1, keepdims=True)
            total = jnp.where(lane == s * len(GRAM) + e, value, total)
    gram[...] = jnp.broadcast_to(total, gram.shape)


def coefficients(numbers):
    def entry(a, b):
        return numbers[(a, b) if a <= b else (b, a)]

    def form(left, right, moved):
        out = None
        for a, u in enumerate(left):
            for b, w in enumerate(right):
                term = u * w * entry(a, b + moved)
                out = term if out is None else out + term
        return out

    one = jnp.ones_like(numbers[(0, 0)])
    residual, direction = [one], [one]
    weights = [jnp.zeros_like(one)] * ITERS
    norm = form(residual, residual, 0)
    for sweep in range(ITERS):
        curve = form(direction, direction, 0) - form(direction, direction, 1)
        step = norm / curve
        weights = [
            w + step * direction[k] if k < len(direction) else w for k, w in enumerate(weights)
        ]
        if sweep + 1 == ITERS:
            break
        image = direction + [jnp.zeros_like(one)]
        image = [image[0]] + [image[k] - direction[k - 1] for k in range(1, len(image))]
        residual = [
            (residual[k] if k < len(residual) else 0.0) - step * image[k] for k in range(len(image))
        ]
        after = form(residual, residual, 0)
        ratio = after / norm
        direction = [
            residual[k] + ratio * direction[k] if k < len(direction) else residual[k]
            for k in range(len(residual))
        ]
        norm = after
    return weights


def finish_kernel(grams, induced, *refs):
    scaleds = refs[:ITERS]
    inverse, result = refs[ITERS : ITERS + 2]
    total = jnp.sum(grams[...], axis=0, keepdims=True)
    rows = []
    for s in range(STATES):
        numbers = {
            pair: total[:, s * len(GRAM) + e : s * len(GRAM) + e + 1]
            for e, pair in enumerate(GRAM)
        }
        weights = coefficients(numbers)
        for k in range(3 * s, 3 * s + 3):
            value = induced[k]
            for w, scaled in zip(weights, scaleds):
                value = value + w * scaled[k]
            rows.append(value)
    done = permuted(inverse[...], rows)
    for k in range(6):
        result[k] = done[k]


def ring(cells, axis):
    count = lax.axis_size(axis)
    if count == 1:
        return [cells], (0, 0, 0)
    below = lax.ppermute(cells, axis, [(i, (i + 1) % count) for i in range(count)])
    if count == 2:
        return [cells, below], (1, 0, 1)
    above = lax.ppermute(cells, axis, [((i + 1) % count, i) for i in range(count)])
    return [below, cells, above], (0, 1, 2)


def neighbours(cells):
    first, place_x = ring(cells, "gx")
    stacked = jnp.stack(first)
    second, place_y = ring(stacked, "gy")
    stacked = jnp.stack(second)
    third, place_z = ring(stacked, "gz")
    where = tuple(
        (place_z[n % 3], (place_y[n // 3 % 3], place_x[n // 9])) for n in range(27)
    )
    return third, where


def shards(coords, charges, dipoles, polar, perturbed, cluster_order, border_clusters,
           tile_list, tile_count):
    atoms = coords.shape[-1]
    clusters = atoms // LANES
    border = border_clusters.shape[-1]
    tile_num = tile_list.shape[-1]
    padded = -(-(clusters + 27 * border) // 8) * 8
    width = STATES * COLS
    qwidth = STATES * QCOLS

    def rows(array, kinds):
        return array.reshape(kinds, clusters, LANES)

    order = cluster_order.reshape(clusters, LANES)
    border_ids = border_clusters.reshape(border)
    tiles = tile_list.reshape(3, tile_num)
    count = tile_count.reshape(1)

    cell = (clusters, LANES)
    place, multi, response, outgoing = call(
        prepare_kernel,
        [((3,) + cell, F32), ((8,) + cell, F32), ((2,) + cell, F32), ((11, border, LANES), F32)],
        [VMEM] * 6 + [SMEM],
    )(rows(coords, 3), rows(charges, 2), rows(dipoles, 6), rows(polar, 2),
      perturbed.reshape(cell), order, border_ids)
    (inverse,) = call(inverse_kernel, [(cell, jnp.int32)], [VMEM])(order)

    halo, where = neighbours(outgoing)
    matrix_shape = (tile_num, 2 * LANES, LANES)
    flat = pltpu.VMEM((padded * width, LANES), F32)
    parts = pltpu.VMEM((padded, 3 * width, LANES), BF16)
    sums = pltpu.VMEM((clusters * width, LANES), F32)
    sources = pltpu.VMEM((6, padded, LANES), F32)
    induced, leaving, matrix, y, selves = call(
        lambda *refs: build_kernel(where, len(halo), *refs),
        [((6,) + cell, F32), ((6, border, LANES), F32), (matrix_shape, BF16),
         ((3, padded, LANES), F32), (cell, F32)],
        [SMEM] * 3 + [VMEM] * (3 + len(halo)),
        [pltpu.VMEM((8, padded, LANES), F32), flat, pltpu.VMEM((padded * qwidth, LANES), F32),
         parts, pltpu.VMEM((padded, 4 * qwidth, LANES), BF16),
         pltpu.VMEM((3, LANES, padded), F32), sums, pltpu.VMEM((clusters * qwidth, LANES), F32)],
    )(tiles, count, border_ids, place, multi, response, *halo)

    own = induced
    plains, scaleds = [], []
    for _ in range(ITERS):
        halo, where = neighbours(leaving)
        plain, own, leaving = call(
            lambda *refs, where=where: step_kernel(where, len(halo), *refs),
            [((6,) + cell, F32), ((6,) + cell, F32), ((6, border, LANES), F32)],
            [SMEM] * 3 + [VMEM] * (5 + len(halo)),
            [sources, flat, parts, sums],
        )(tiles, count, border_ids, response, y, selves, matrix, own, *halo)
        plains.append(plain)
        scaleds.append(own)
    halo, where = neighbours(leaving)
    (gram,) = call(
        lambda *refs: last_kernel(where, len(halo), border, *refs),
        [((8, LANES), F32)],
        [SMEM] * 2 + [VMEM] * (4 + 2 * ITERS + len(halo)),
        [sources, flat, parts, sums],
    )(tiles, count, response, y, selves, matrix, *plains, *scaleds, *halo)

    devices = 1
    for axis in AXES:
        devices *= lax.axis_size(axis)
    sent = jnp.broadcast_to(gram[:1], (devices, LANES))
    grams = lax.all_to_all(sent, AXES, 0, 0, tiled=True)
    (result,) = call(
        finish_kernel, [((6,) + cell, F32)], [VMEM] * (3 + ITERS)
    )(grams, induced, *scaleds, inverse)
    return result.reshape(6, 1, 1, 1, atoms)


def solution(mesh):
    wide = P(None, "gx", "gy", "gz", None)
    brick = P("gx", "gy", "gz", None)
    placed = (wide, wide, wide, wide, brick, brick, brick, wide, P("gx", "gy", "gz"))
    return jax.shard_map(
        shards, mesh=mesh, in_specs=placed, out_specs=wide, check_vma=False
    )
```

```python
import jax
import jax.numpy as jnp
from jax import lax
from jax.experimental import pallas as pl
from jax.experimental.pallas import tpu as pltpu
from jax.sharding import PartitionSpec as P

ITERS = 3
LANES = 128
BRICK = 6.0
STATES = 2
WIDTH = STATES * 3 * 8
QWIDTH = STATES * 8
PARTS = 12
UNROLL = 16
WEIGH_UNROLL = 8
HIDDEN = 4_000_000_000
F32 = jnp.float32
BF16 = jnp.bfloat16
AXES = ("gx", "gy", "gz")
GRAM = tuple((a, b) for a in range(ITERS) for b in range(a, ITERS + 1))

VMEM = pl.BlockSpec(memory_space=pltpu.VMEM)
SMEM = pl.BlockSpec(memory_space=pltpu.SMEM)


def thirds(value):
    high = value.astype(BF16).astype(F32)
    rest = value - high
    middle = rest.astype(BF16).astype(F32)
    return high, middle, rest - middle


def call(kernel, shapes, spaces, scratch=(), limit=8, outs=None, flops=None):
    cost = None
    if flops is not None:
        cost = pl.CostEstimate(flops=flops, bytes_accessed=0, transcendentals=0)
    return pl.pallas_call(
        kernel,
        out_shape=[jax.ShapeDtypeStruct(shape, dtype) for shape, dtype in shapes],
        in_specs=spaces,
        out_specs=outs or [VMEM] * len(shapes),
        scratch_shapes=list(scratch),
        cost_estimate=cost,
        compiler_params=pltpu.CompilerParams(vmem_limit_bytes=limit << 20),
    )


def lane_take(rows, lane):
    return jnp.take_along_axis(rows, lane, axis=1, mode="promise_in_bounds")


def permuted(order, rows):
    chunks = order.shape[0]
    lane, chunk = order & (LANES - 1), order >> 7
    picked = [jnp.zeros(order.shape, F32) for _ in rows]
    for c in range(chunks):
        here = chunk == c
        for k, row in enumerate(rows):
            taken = lane_take(jnp.broadcast_to(row[c : c + 1, :], order.shape), lane)
            picked[k] = jnp.where(here, taken, picked[k])
    return picked


def prepare_kernel(packed, place, multi, response, outgoing, order):
    coords, charges, dipoles, polar = (
        [packed[k] for k in range(first, end)]
        for first, end in ((0, 3), (3, 5), (5, 11), (11, 13))
    )
    changed = packed[13] == 1.0
    order[...] = packed[14].astype(jnp.int32)
    lane = lax.broadcasted_iota(jnp.int32, (1, LANES), 1)
    ids = packed[15, 0:1, :]
    rows = [coord - 0.5 * BRICK for coord in coords]
    rows += [charges[0], jnp.where(changed, charges[1], charges[0])]
    rows += dipoles[:3]
    rows += [jnp.where(changed, dipoles[3 + k], dipoles[k]) for k in range(3)]
    rows += [polar[0], jnp.where(changed, polar[1], polar[0])]
    done = permuted(order[...], rows)
    for k in range(3):
        place[k] = done[k]
    for k in range(8):
        multi[k] = done[3 + k]
    for k in range(2):
        response[k] = done[11 + k]
    for b in range(outgoing.shape[1]):
        chosen = jnp.sum(jnp.where(lane == b, ids, 0.0)).astype(jnp.int32)
        row = pl.ds(chosen, 1)
        for k in range(3):
            outgoing[k, pl.ds(b, 1), :] = place[k, row, :]
        for k in range(8):
            outgoing[3 + k, pl.ds(b, 1), :] = multi[k, row, :]


def inverse_kernel(order, inverse):
    clusters = order.shape[0]
    column = jnp.transpose(order[...].astype(F32))
    lanes = lax.broadcasted_iota(jnp.int32, (8, LANES), 1).astype(F32)
    subs = lax.broadcasted_iota(jnp.int32, (8, LANES), 0).astype(F32)
    total = [jnp.zeros((8, LANES), F32) for _ in range(clusters)]
    for c in range(clusters):
        for g in range(LANES // 8):
            value = jnp.broadcast_to(column[8 * g : 8 * g + 8, c : c + 1], (8, LANES))
            slot = subs + float(c * LANES + 8 * g)
            for a in range(clusters):
                total[a] = jnp.where(value == lanes + float(a * LANES), slot, total[a])
    for a in range(clusters):
        inverse[a : a + 1, :] = jnp.sum(total[a], axis=0, keepdims=True).astype(jnp.int32)


def collect(target, first, own, halo, where, border, moves=None):
    kinds, padded = target.shape[0], target.shape[1]
    clusters = own.shape[1]
    base13 = clusters + 13 * border
    used = clusters + 27 * border
    for k in range(kinds):
        target[k, 0:clusters, :] = own[first + k]
        target[k, base13 : base13 + border, :] = jnp.zeros((border, LANES), F32)
        if padded > used:
            target[k, used:padded, :] = jnp.zeros((padded - used, LANES), F32)
    for slot in range(27):
        if slot == 13:
            continue
        ref, index = where[slot]
        base = clusters + slot * border
        for k in range(kinds):
            piece = halo[ref][index + (first + k,)]
            if moves is not None:
                piece = piece + moves[slot][k]
            target[k, base : base + border, :] = piece


def spread_row(ref, k, row):
    return jnp.broadcast_to(ref[k, pl.ds(row, 1), :], (8, LANES))


def write_factors(factors, y):
    sub = lax.broadcasted_iota(jnp.int32, (8, LANES), 0)
    axis_of = [jnp.logical_or(sub == 1 + k, sub == 4 + k) for k in range(3)]
    outer = jnp.logical_and(sub >= 4, sub < 7)
    unit = jnp.where(sub == 0, 1.0, 0.0).astype(F32)

    def one(r, carry):
        ys = [spread_row(y, k, r) for k in range(3)]
        far = ys[0] * ys[0] + ys[1] * ys[1] + ys[2] * ys[2]
        line = unit
        for k in range(3):
            line = jnp.where(axis_of[k], ys[k], line)
        for b in range(3):
            value = line * jnp.where(outer, 3.0 * ys[b], 1.0)
            factors[r, b] = value - jnp.where(sub == 4 + b, far, 0.0)
        return carry

    lax.fori_loop(0, y.shape[1], one, None, unroll=4)


def columns(factors, sources, row):
    block = jnp.concatenate(
        [factors[row, k % 3] * spread_row(sources, k, row) for k in range(3 * STATES)], axis=0
    )
    return jnp.concatenate(thirds(block), axis=0).astype(BF16)


def charge_columns(factors, charges, row):
    line = factors[row, 0]
    block = jnp.concatenate([line * spread_row(charges, s, row) for s in range(STATES)], axis=0)
    return jnp.concatenate(thirds(block), axis=0).astype(BF16)


def apply(left, right, width):
    both = jnp.concatenate([right[0:LANES], right[LANES:]], axis=1)
    product = lax.dot_general(
        jnp.concatenate([left, left], axis=1), both, (((1,), (1,)), ((), ())),
        preferred_element_type=F32,
    )
    return product[0:width] + product[width : 2 * width] + product[2 * width : 3 * width]


def add_tile(sums, recv, width, value):
    at = pl.ds(pl.multiple_of(recv * width, 8), width)
    sums[at, :] += value


def combine(sums, x, v, selves):
    clusters = x[0].shape[0]
    reach = x[0] * x[0] + x[1] * x[1] + x[2] * x[2] + 1.0
    fields = []
    for s in range(STATES):
        def col(b, c):
            return sums[pl.ds((3 * s + b) * 8 + c, clusters, stride=WIDTH), :]

        plain = [col(b, 0) for b in range(3)]
        cross = [[col(b, 1 + k) for k in range(3)] for b in range(3)]
        outer = [col(0, 4 + b) + col(1, 4 + b) + col(2, 4 + b) for b in range(3)]
        inner = x[0] * plain[0] + x[1] * plain[1] + x[2] * plain[2]
        inner = 3.0 * (inner - (cross[0][0] + cross[1][1] + cross[2][2]))
        for b in range(3):
            value = x[b] * inner - reach * plain[b] + outer[b]
            for k in range(3):
                value = value + x[k] * (2.0 * cross[b][k] - 3.0 * cross[k][b])
            fields.append(value + selves * v[3 * s + b])
    return fields


def receiver_features(place, c):
    sub = lax.broadcasted_iota(jnp.int32, (8, LANES), 0)
    zero = jnp.zeros((8, LANES), F32)
    unit = jnp.where(sub == 0, 1.0, 0.0).astype(F32)
    xs = [spread_row(place, k, c) for k in range(3)]
    groups = []
    for x in xs:
        high, middle, low = thirds(-2.0 * x)
        first = jnp.where(sub == 0, high, zero)
        second = jnp.where(sub == 1, middle, first)
        groups += [jnp.where(sub == 2, low, second), second, first]
    groups += [unit, unit, unit]
    high, middle, low = thirds(xs[0] * xs[0] + xs[1] * xs[1] + xs[2] * xs[2])
    groups.append(
        jnp.where(sub == 0, high, jnp.where(sub == 1, middle, jnp.where(sub == 2, low, zero)))
    )
    groups += [zero] * (LANES // 8 - len(groups))
    return jnp.concatenate(groups, axis=0).astype(BF16)


def write_parts(pieces, y):
    for g in range(y.shape[1] // 8):
        at = slice(8 * g, 8 * g + 8)
        ys = [y[k, at, :] for k in range(3)]
        ys.append(ys[0] * ys[0] + ys[1] * ys[1] + ys[2] * ys[2] + 1.0)
        for k in range(4):
            for p, part in enumerate(thirds(ys[k])):
                pieces[3 * k + p, at, :] = part


def source_features(pieces, row):
    groups = [spread_row(pieces, k, row) for k in range(PARTS)]
    groups.append(jnp.ones((8, LANES), F32))
    groups += [jnp.zeros((8, LANES), F32)] * (LANES // 8 - len(groups))
    return jnp.concatenate(groups, axis=0).astype(BF16)


def plan_kernel(tiles, count, border_ids, near, rest, sizes, selves, flags, pairs):
    clusters = selves.shape[0]
    border = border_ids.shape[0]
    tile_num = tiles.shape[1]
    dummy = clusters + 13 * border
    for c in range(clusters):
        flags[c] = 0
        pairs[c] = 0
    for b in range(border):
        flags[border_ids[b]] = 1

    def place_tile(t, ends):
        recv, slot, source = tiles[0, t], tiles[1, t], tiles[2, t]
        row = jnp.where(slot == 13, source, clusters + slot * border + source)
        used = (t < count[0]).astype(jnp.int32)
        seen = flags[recv]
        for which, target in enumerate((near, rest)):
            target[0, ends[which]] = recv
            target[1, ends[which]] = row
        same = jnp.logical_and(slot == 13, source == recv).astype(jnp.int32)
        pairs[recv] = pairs[recv] + used * same
        return ends[0] + used * seen, ends[1] + used * (1 - seen)

    ends = lax.fori_loop(0, tile_num, place_tile, (jnp.int32(0), jnp.int32(0)))
    for which, target in enumerate((near, rest)):
        for u in range(UNROLL):
            target[0, ends[which] + u] = 0
            target[1, ends[which] + u] = dummy
        sizes[which] = (ends[which] + UNROLL - 1) // UNROLL
    sizes[2] = (sizes[1] + 1) // 2
    for c in range(clusters):
        selves[c : c + 1, :] = jnp.full((1, LANES), pairs[c].astype(F32))


def turn_kernel(place, turned):
    eye = lax.broadcasted_iota(jnp.int32, (LANES, LANES), 0) == lax.broadcasted_iota(
        jnp.int32, (LANES, LANES), 1
    )
    eye = jnp.where(eye, 1.0, 0.0).astype(BF16)

    def turn(c, carry):
        turned[c] = lax.dot_general(
            eye, receiver_features(place, c), (((1,), (1,)), ((), ())),
            preferred_element_type=F32,
        ).astype(BF16)
        return carry

    lax.fori_loop(0, place.shape[1], turn, None, unroll=8)


def over_tiles(groups, body, unroll=UNROLL):
    def one(i, carry):
        for u in range(unroll):
            body(i * unroll + u)
        return carry

    first, end = groups if isinstance(groups, tuple) else (0, groups)
    lax.fori_loop(first * (UNROLL // unroll), end * (UNROLL // unroll), one, None)


def weigh_tiles(tiles, groups, turned, pieces, matrix, cubes):
    def one(t):
        recv, row = tiles[0, t], tiles[1, t]
        squared = jnp.dot(
            turned[recv], source_features(pieces, row), preferred_element_type=F32
        )
        inverse = lax.rsqrt(squared)
        second = inverse * inverse
        g3 = second * inverse
        g5 = g3 * second
        for target, value in ((matrix, g5), (cubes, g3)):
            high = value.astype(BF16)
            target[t, 0:LANES, :] = high
            target[t, LANES:, :] = (value - high.astype(F32)).astype(BF16)

    over_tiles(groups, one, WEIGH_UNROLL)


def apply_tiles(tiles, groups, factors, sources, matrix, sums, charges=None, cubes=None, sums_q=None):
    def one(t):
        recv, row = tiles[0, t], tiles[1, t]
        add_tile(sums, recv, WIDTH, apply(columns(factors, sources, row), matrix[t], WIDTH))
        if cubes is not None:
            left = charge_columns(factors, charges, row)
            add_tile(sums_q, recv, QWIDTH, apply(left, cubes[t], QWIDTH))

    over_tiles(groups, one)


def permanent(sums, sums_q, place, multi, selves):
    clusters = place.shape[1]
    x = [place[k] for k in range(3)]
    fields = combine(sums, x, [multi[2 + k] for k in range(6)], selves[...])
    for s in range(STATES):
        def col(c):
            return sums_q[pl.ds(s * 8 + c, clusters, stride=QWIDTH), :]

        whole = col(0)
        for b in range(3):
            fields[3 * s + b] = fields[3 * s + b] + (x[b] * whole - col(1 + b))
    return fields


class Stack:
    def __init__(self, rows):
        self.rows = rows
        self.shape = (len(rows),) + rows[0].shape

    def __getitem__(self, k):
        return self.rows[k]


def send_border(values, held, outgoing, border_ids):
    for k, value in enumerate(values):
        held[k] = value
    for b in range(outgoing.shape[1]):
        row = pl.ds(border_ids[b], 1)
        for k in range(len(values)):
            outgoing[k, pl.ds(b, 1), :] = held[k, row, :]


def first_near_kernel(where, parts_of, *refs):
    tiles, sizes, border_ids, place, multi, response, turned, selves = refs[:8]
    halo = refs[8 : 8 + parts_of]
    (outgoing, matrix, factors, pieces, moments, charges, sums, sums_q,
     y, cubes, held) = refs[8 + parts_of :]
    border = outgoing.shape[1]
    moves = [
        tuple(BRICK * o for o in (slot // 9 - 1, slot // 3 % 3 - 1, slot % 3 - 1))
        for slot in range(27)
    ]
    own = Stack([place[k] for k in range(3)] + [multi[k] for k in range(8)])
    collect(y, 0, own, halo, where, border, moves)
    collect(charges, 3, own, halo, where, border)
    collect(moments, 5, own, halo, where, border)
    write_factors(factors, y)
    write_parts(pieces, y)
    sums[...] = jnp.zeros_like(sums)
    sums_q[...] = jnp.zeros_like(sums_q)
    weigh_tiles(tiles, sizes[0], turned, pieces, matrix, cubes)
    apply_tiles(tiles, sizes[0], factors, moments, matrix, sums, charges, cubes, sums_q)
    fields = permanent(sums, sums_q, place, multi, selves)
    send_border(
        [response[k // 3] * fields[k] for k in range(6)], held, outgoing, border_ids
    )


def first_weigh_kernel(tiles, sizes, turned, pieces, matrix, cubes):
    weigh_tiles(tiles, sizes[1], turned, pieces, matrix, cubes)


def first_rest_kernel(tiles, sizes, place, multi, response, selves, factors,
                      moments, charges, matrix, cubes, sums_in, sums_q_in, induced, sums, sums_q):
    sums[...] = sums_in[...]
    sums_q[...] = sums_q_in[...]
    apply_tiles(tiles, sizes[1], factors, moments, matrix, sums, charges, cubes, sums_q)
    fields = permanent(sums, sums_q, place, multi, selves)
    for k in range(6):
        induced[k] = response[k // 3] * fields[k]


def near_kernel(where, parts_of, *refs):
    tiles, sizes, border_ids, place, response, selves, factors, matrix, own = refs[:9]
    halo = refs[9 : 9 + parts_of]
    outgoing, sources, sums, held = refs[9 + parts_of :]
    collect(sources, 0, own, halo, where, outgoing.shape[1])
    sums[...] = jnp.zeros_like(sums)
    apply_tiles(tiles, sizes[0], factors, sources, matrix, sums)
    x = [place[k] for k in range(3)]
    fields = combine(sums, x, [own[k] for k in range(6)], selves[...])
    send_border(
        [response[k // 3] * fields[k] for k in range(6)], held, outgoing, border_ids
    )


def middle_kernel(tiles, sizes, factors, matrix, sources, sums_in, sums):
    sums[...] = sums_in[...]
    apply_tiles(tiles, sizes[2], factors, sources, matrix, sums)


def rest_kernel(tiles, sizes, place, response, selves, factors, matrix, own, sources, sums_in,
                plain, scaled, sums):
    sums[...] = sums_in[...]
    apply_tiles(tiles, (sizes[2], sizes[1]), factors, sources, matrix, sums)
    x = [place[k] for k in range(3)]
    fields = combine(sums, x, [own[k] for k in range(6)], selves[...])
    for k in range(6):
        plain[k] = fields[k]
        scaled[k] = response[k // 3] * fields[k]


def last_kernel(where, parts_of, border, *refs):
    near, rest, sizes, place, response, selves, factors, matrix_near, matrix_rest = refs[:9]
    plains = refs[9 : 9 + ITERS]
    scaleds = refs[9 + ITERS : 9 + 2 * ITERS]
    base = 9 + 2 * ITERS
    halo = refs[base : base + parts_of]
    gram, sources, sums = refs[base + parts_of :]
    own = scaleds[-1]
    collect(sources, 0, own, halo, where, border)
    sums[...] = jnp.zeros_like(sums)
    apply_tiles(near, sizes[0], factors, sources, matrix_near, sums)
    apply_tiles(rest, sizes[1], factors, sources, matrix_rest, sums)
    x = [place[k] for k in range(3)]
    fields = combine(sums, x, [own[k] for k in range(6)], selves[...])
    lane = lax.broadcasted_iota(jnp.int32, (1, LANES), 1)
    total = jnp.zeros((1, LANES), F32)
    for s in range(STATES):
        for e, (a, b) in enumerate(GRAM):
            sum_of = None
            for k in range(3 * s, 3 * s + 3):
                right = scaleds[b][k] if b < ITERS else response[s] * fields[k]
                term = plains[a][k] * right
                sum_of = term if sum_of is None else sum_of + term
            value = jnp.sum(jnp.sum(sum_of, axis=0, keepdims=True), axis=1, keepdims=True)
            total = jnp.where(lane == s * len(GRAM) + e, value, total)
    gram[...] = jnp.broadcast_to(total, gram.shape)


def coefficients(numbers):
    def entry(a, b):
        return numbers[(a, b) if a <= b else (b, a)]

    def form(left, right, moved):
        out = None
        for a, u in enumerate(left):
            for b, w in enumerate(right):
                term = u * w * entry(a, b + moved)
                out = term if out is None else out + term
        return out

    one = jnp.ones_like(numbers[(0, 0)])
    residual, direction = [one], [one]
    weights = [jnp.zeros_like(one)] * ITERS
    norm = form(residual, residual, 0)
    for sweep in range(ITERS):
        curve = form(direction, direction, 0) - form(direction, direction, 1)
        step = norm / curve
        weights = [
            w + step * direction[k] if k < len(direction) else w for k, w in enumerate(weights)
        ]
        if sweep + 1 == ITERS:
            break
        image = direction + [jnp.zeros_like(one)]
        image = [image[0]] + [image[k] - direction[k - 1] for k in range(1, len(image))]
        residual = [
            (residual[k] if k < len(residual) else 0.0) - step * image[k] for k in range(len(image))
        ]
        after = form(residual, residual, 0)
        ratio = after / norm
        direction = [
            residual[k] + ratio * direction[k] if k < len(direction) else residual[k]
            for k in range(len(residual))
        ]
        norm = after
    return weights


def finish_kernel(grams, induced, *refs):
    scaleds = refs[:ITERS]
    inverse, result = refs[ITERS : ITERS + 2]
    total = jnp.sum(grams[...], axis=0, keepdims=True)
    rows = []
    for s in range(STATES):
        numbers = {
            pair: total[:, s * len(GRAM) + e : s * len(GRAM) + e + 1]
            for e, pair in enumerate(GRAM)
        }
        weights = coefficients(numbers)
        for k in range(3 * s, 3 * s + 3):
            value = induced[k]
            for w, scaled in zip(weights, scaleds):
                value = value + w * scaled[k]
            rows.append(value)
    done = permuted(inverse[...], rows)
    for k in range(6):
        result[k] = done[k]


def ring(cells, axis):
    count = lax.axis_size(axis)
    if count == 1:
        return [cells], (0, 0, 0)
    below = lax.ppermute(cells, axis, [(i, (i + 1) % count) for i in range(count)])
    if count == 2:
        return [cells, below], (1, 0, 1)
    above = lax.ppermute(cells, axis, [((i + 1) % count, i) for i in range(count)])
    return [below, cells, above], (0, 1, 2)


def neighbours(cells, beside):
    first, place_x = ring(cells, "gx")
    stacked, *beside = lax.optimization_barrier((jnp.stack(first), *beside))
    second, place_y = ring(stacked, "gy")
    stacked = jnp.stack(second)
    third, place_z = ring(stacked, "gz")
    where = tuple(
        (place_z[n % 3], (place_y[n // 3 % 3], place_x[n // 9])) for n in range(27)
    )
    return third, where, beside


def shards(coords, charges, dipoles, polar, perturbed, cluster_order, border_clusters,
           tile_list, tile_count):
    atoms = coords.shape[-1]
    clusters = atoms // LANES
    border = border_clusters.shape[-1]
    tile_num = tile_list.shape[-1]
    padded = -(-(clusters + 27 * border) // LANES) * LANES

    border_ids = border_clusters.reshape(border)
    tiles = tile_list.reshape(3, tile_num)
    count = tile_count.reshape(1)
    devices = 1
    for axis in AXES:
        devices *= lax.axis_size(axis)

    cell = (clusters, LANES)
    vector = ((6,) + cell, F32)
    leave = ((6, border, LANES), F32)
    listed = -(-tile_num // UNROLL) * UNROLL
    matrix = ((listed, 2 * LANES, LANES), BF16)
    table = ((6, padded, LANES), F32)
    sums = ((clusters * WIDTH, LANES), F32)
    sums_q = ((clusters * QWIDTH, LANES), F32)
    listing = ((2, listed + UNROLL), jnp.int32)

    whole, at = {}, 0
    for array in (coords, charges, dipoles, polar, perturbed, cluster_order, border_ids):
        array = array.reshape((1, 1, border) if array.ndim == 1 else (-1,) + cell)
        kinds = array.shape[0]
        sides = [(at, 16 - at - kinds)] + [(0, n - k) for n, k in zip(cell, array.shape[1:])]
        array = jnp.pad(array, sides)
        whole[array.dtype] = whole[array.dtype] + array if array.dtype in whole else array
        at += kinds
    whole = sum(part.astype(F32) for part in whole.values())
    place, multi, response, outgoing, order = call(
        prepare_kernel,
        [((3,) + cell, F32), ((8,) + cell, F32), ((2,) + cell, F32), ((11, border, LANES), F32),
         (cell, jnp.int32)],
        [VMEM],
    )(whole)
    near, rest, sizes, selves = call(
        plan_kernel,
        [listing, listing, ((3,), jnp.int32), (cell, F32)],
        [SMEM] * 3,
        [pltpu.SMEM((clusters,), jnp.int32)] * 2,
        outs=[SMEM] * 3 + [VMEM],
        flops=HIDDEN,
    )(tiles, count, border_ids)
    (turned,) = call(
        turn_kernel, [((clusters, LANES, LANES), BF16)], [VMEM], flops=HIDDEN
    )(place)
    (inverse,) = call(inverse_kernel, [(cell, jnp.int32)], [VMEM], flops=HIDDEN)(order)

    halo, where, (turned,) = neighbours(outgoing, (turned,))
    (leaving, matrix_near, factors, pieces, moments, charge_rows, partial, partial_q) = call(
        lambda *refs: first_near_kernel(where, len(halo), *refs),
        [leave, matrix, ((padded, 3, 8, LANES), F32), ((PARTS, padded, LANES), F32), table,
         ((2, padded, LANES), F32), sums, sums_q],
        [SMEM] * 3 + [VMEM] * (5 + len(halo)),
        [pltpu.VMEM((3, padded, LANES), F32), pltpu.VMEM(*matrix), pltpu.VMEM(*vector)],
        16,
    )(near, sizes, border_ids, place, multi, response, turned, selves, *halo)
    matrix_rest, cubes = call(
        first_weigh_kernel, [matrix, matrix], [SMEM] * 2 + [VMEM] * 2, flops=HIDDEN
    )(rest, sizes, turned, pieces)
    halo, where, (matrix_rest, cubes) = neighbours(leaving, (matrix_rest, cubes))
    (induced,) = call(
        first_rest_kernel, [vector], [SMEM] * 2 + [VMEM] * 11,
        [pltpu.VMEM(*sums), pltpu.VMEM(*sums_q)], flops=HIDDEN,
    )(rest, sizes, place, multi, response, selves, factors, moments, charge_rows,
      matrix_rest, cubes, partial, partial_q)

    own = induced
    plains, scaleds = [], []
    for _ in range(ITERS):
        leaving, sources, partial = call(
            lambda *refs, where=where, parts=len(halo): near_kernel(where, parts, *refs),
            [leave, table, sums], [SMEM] * 3 + [VMEM] * (6 + len(halo)),
            [pltpu.VMEM(*vector)],
        )(near, sizes, border_ids, place, response, selves, factors, matrix_near, own, *halo)
        (partial,) = call(
            middle_kernel, [sums], [SMEM] * 2 + [VMEM] * 4, flops=HIDDEN
        )(rest, sizes, factors, matrix_rest, sources, partial)
        halo, where, (partial,) = neighbours(leaving, (partial,))
        plain, own = call(
            rest_kernel, [vector, vector], [SMEM] * 2 + [VMEM] * 8, [pltpu.VMEM(*sums)],
            flops=HIDDEN,
        )(rest, sizes, place, response, selves, factors, matrix_rest, own, sources, partial)
        plains.append(plain)
        scaleds.append(own)
    (gram,) = call(
        lambda *refs: last_kernel(where, len(halo), border, *refs),
        [((devices, LANES), F32)],
        [SMEM] * 3 + [VMEM] * (6 + 2 * ITERS + len(halo)),
        [pltpu.VMEM(*table), pltpu.VMEM(*sums)],
    )(near, rest, sizes, place, response, selves, factors, matrix_near, matrix_rest,
      *plains, *scaleds, *halo)

    grams = lax.all_to_all(gram, AXES, 0, 0, tiled=True)
    (result,) = call(
        finish_kernel, [vector], [VMEM] * (3 + ITERS)
    )(grams, induced, *scaleds, inverse)
    return result.reshape(6, 1, 1, 1, atoms)


def solution(mesh):
    wide = P(None, "gx", "gy", "gz", None)
    brick = P("gx", "gy", "gz", None)
    placed = (wide, wide, wide, wide, brick, brick, brick, wide, P("gx", "gy", "gz"))
    return jax.shard_map(
        shards, mesh=mesh, in_specs=placed, out_specs=wide, check_vma=False
    )
```

```python
import jax
import jax.numpy as jnp
from jax import lax
from jax.experimental import pallas as pl
from jax.experimental.pallas import tpu as pltpu
from jax.sharding import PartitionSpec as P

ITERS = 3
LANES = 128
BRICK = 6.0
STATES = 2
WIDTH = STATES * 3 * 8
QWIDTH = STATES * 4
PARTS = 12
UNROLL = 16
WIDE = 32
HIDDEN = 4_000_000_000
F32 = jnp.float32
BF16 = jnp.bfloat16
AXES = ("gx", "gy", "gz")
GRAM = tuple((a, b) for a in range(ITERS) for b in range(a, ITERS + 1))

VMEM = pl.BlockSpec(memory_space=pltpu.VMEM)
SMEM = pl.BlockSpec(memory_space=pltpu.SMEM)


def thirds(value):
    high = value.astype(BF16).astype(F32)
    rest = value - high
    middle = rest.astype(BF16).astype(F32)
    return high, middle, rest - middle


def call(kernel, shapes, spaces, scratch=(), limit=8, outs=None, flops=None):
    cost = None
    if flops is not None:
        cost = pl.CostEstimate(flops=flops, bytes_accessed=0, transcendentals=0)
    return pl.pallas_call(
        kernel,
        out_shape=[jax.ShapeDtypeStruct(shape, dtype) for shape, dtype in shapes],
        in_specs=spaces,
        out_specs=outs or [VMEM] * len(shapes),
        scratch_shapes=list(scratch),
        cost_estimate=cost,
        compiler_params=pltpu.CompilerParams(vmem_limit_bytes=limit << 20),
    )


def lane_take(rows, lane):
    return jnp.take_along_axis(rows, lane, axis=1, mode="promise_in_bounds")


def permuted(order, rows):
    chunks = order.shape[0]
    lane, chunk = order & (LANES - 1), order >> 7
    picked = [jnp.zeros(order.shape, F32) for _ in rows]
    for c in range(chunks):
        here = chunk == c
        for k, row in enumerate(rows):
            taken = lane_take(jnp.broadcast_to(row[c : c + 1, :], order.shape), lane)
            picked[k] = jnp.where(here, taken, picked[k])
    return picked


def prepare_kernel(packed, place, multi, response, outgoing, order):
    coords, charges, dipoles, polar = (
        [packed[k] for k in range(first, end)]
        for first, end in ((0, 3), (3, 5), (5, 11), (11, 13))
    )
    changed = packed[13] == 1.0
    order[...] = packed[14].astype(jnp.int32)
    lane = lax.broadcasted_iota(jnp.int32, (1, LANES), 1)
    ids = packed[15, 0:1, :]
    rows = [coord - 0.5 * BRICK for coord in coords]
    rows += [charges[0], jnp.where(changed, charges[1], charges[0])]
    rows += dipoles[:3]
    rows += [jnp.where(changed, dipoles[3 + k], dipoles[k]) for k in range(3)]
    rows += [polar[0], jnp.where(changed, polar[1], polar[0])]
    done = permuted(order[...], rows)
    for k in range(3):
        place[k] = done[k]
    for k in range(8):
        multi[k] = done[3 + k]
    for k in range(2):
        response[k] = done[11 + k]
    for b in range(outgoing.shape[1]):
        chosen = jnp.sum(jnp.where(lane == b, ids, 0.0)).astype(jnp.int32)
        row = pl.ds(chosen, 1)
        for k in range(3):
            outgoing[k, pl.ds(b, 1), :] = place[k, row, :]
        for k in range(8):
            outgoing[3 + k, pl.ds(b, 1), :] = multi[k, row, :]


def inverse_kernel(order, inverse):
    clusters = order.shape[0]
    column = jnp.transpose(order[...].astype(F32))
    lanes = lax.broadcasted_iota(jnp.int32, (8, LANES), 1).astype(F32)
    subs = lax.broadcasted_iota(jnp.int32, (8, LANES), 0).astype(F32)
    total = [jnp.zeros((8, LANES), F32) for _ in range(clusters)]
    for c in range(clusters):
        for g in range(LANES // 8):
            value = jnp.broadcast_to(column[8 * g : 8 * g + 8, c : c + 1], (8, LANES))
            slot = subs + float(c * LANES + 8 * g)
            for a in range(clusters):
                total[a] = jnp.where(value == lanes + float(a * LANES), slot, total[a])
    for a in range(clusters):
        inverse[a : a + 1, :] = jnp.sum(total[a], axis=0, keepdims=True).astype(jnp.int32)


def collect(target, first, own, halo, where, border, moves=None):
    kinds, padded = target.shape[0], target.shape[1]
    clusters = own.shape[1]
    base13 = clusters + 13 * border
    used = clusters + 27 * border
    for k in range(kinds):
        target[k, 0:clusters, :] = own[first + k]
        target[k, base13 : base13 + border, :] = jnp.zeros((border, LANES), F32)
        if padded > used:
            target[k, used:padded, :] = jnp.zeros((padded - used, LANES), F32)
    for slot in range(27):
        if slot == 13:
            continue
        ref, index = where[slot]
        base = clusters + slot * border
        for k in range(kinds):
            piece = halo[ref][index + (first + k,)]
            if moves is not None:
                piece = piece + moves[slot][k]
            target[k, base : base + border, :] = piece


def spread_row(ref, k, row):
    return jnp.broadcast_to(ref[k, pl.ds(row, 1), :], (8, LANES))


def write_factors(factors, y):
    sub = lax.broadcasted_iota(jnp.int32, (8, LANES), 0)
    axis_of = [jnp.logical_or(sub == 1 + k, sub == 4 + k) for k in range(3)]
    outer = jnp.logical_and(sub >= 4, sub < 7)
    unit = jnp.where(sub == 0, 1.0, 0.0).astype(F32)

    def one(r, carry):
        ys = [spread_row(y, k, r) for k in range(3)]
        far = ys[0] * ys[0] + ys[1] * ys[1] + ys[2] * ys[2]
        line = unit
        for k in range(3):
            line = jnp.where(axis_of[k], ys[k], line)
        for b in range(3):
            value = line * jnp.where(outer, 3.0 * ys[b], 1.0)
            factors[r, b] = value - jnp.where(sub == 4 + b, far, 0.0)
        line = jnp.ones_like(line)
        for k in range(3):
            line = jnp.where(sub % 4 == 1 + k, ys[k], line)
        factors[r, 3] = line
        return carry

    lax.fori_loop(0, y.shape[1], one, None, unroll=4)


def columns(factors, sources, row):
    block = jnp.concatenate(
        [factors[row, k % 3] * spread_row(sources, k, row) for k in range(3 * STATES)], axis=0
    )
    return jnp.concatenate(thirds(block), axis=0).astype(BF16)


def charge_columns(factors, charges, row):
    sub = lax.broadcasted_iota(jnp.int32, (8, LANES), 0)
    both = jnp.where(sub < 4, spread_row(charges, 0, row), spread_row(charges, 1, row))
    pieces = thirds(factors[row, 3] * both) + (jnp.zeros_like(both),)
    return jnp.concatenate(pieces, axis=0).astype(BF16)


def apply(left, right, width):
    both = jnp.concatenate([right[0:LANES], right[LANES:]], axis=1)
    product = lax.dot_general(
        jnp.concatenate([left, left], axis=1), both, (((1,), (1,)), ((), ())),
        preferred_element_type=F32,
    )
    return product[0:width] + product[width : 2 * width] + product[2 * width : 3 * width]


def add_tile(sums, recv, width, value):
    at = pl.ds(pl.multiple_of(recv * width, 8), width)
    sums[at, :] += value


def combine(sums, x, v, selves):
    clusters = x[0].shape[0]
    reach = x[0] * x[0] + x[1] * x[1] + x[2] * x[2] + 1.0
    fields = []
    for s in range(STATES):
        def col(b, c):
            return sums[pl.ds((3 * s + b) * 8 + c, clusters, stride=WIDTH), :]

        plain = [col(b, 0) for b in range(3)]
        cross = [[col(b, 1 + k) for k in range(3)] for b in range(3)]
        outer = [col(0, 4 + b) + col(1, 4 + b) + col(2, 4 + b) for b in range(3)]
        inner = x[0] * plain[0] + x[1] * plain[1] + x[2] * plain[2]
        inner = 3.0 * (inner - (cross[0][0] + cross[1][1] + cross[2][2]))
        for b in range(3):
            value = x[b] * inner - reach * plain[b] + outer[b]
            for k in range(3):
                value = value + x[k] * (2.0 * cross[b][k] - 3.0 * cross[k][b])
            fields.append(value + selves * v[3 * s + b])
    return fields


def receiver_features(place, c):
    sub = lax.broadcasted_iota(jnp.int32, (8, LANES), 0)
    zero = jnp.zeros((8, LANES), F32)
    unit = jnp.where(sub == 0, 1.0, 0.0).astype(F32)
    xs = [spread_row(place, k, c) for k in range(3)]
    groups = []
    for x in xs:
        high, middle, low = thirds(-2.0 * x)
        first = jnp.where(sub == 0, high, zero)
        second = jnp.where(sub == 1, middle, first)
        groups += [jnp.where(sub == 2, low, second), second, first]
    groups += [unit, unit, unit]
    high, middle, low = thirds(xs[0] * xs[0] + xs[1] * xs[1] + xs[2] * xs[2])
    groups.append(
        jnp.where(sub == 0, high, jnp.where(sub == 1, middle, jnp.where(sub == 2, low, zero)))
    )
    groups += [zero] * (LANES // 8 - len(groups))
    return jnp.concatenate(groups, axis=0).astype(BF16)


def write_parts(pieces, y):
    for g in range(y.shape[1] // 8):
        at = slice(8 * g, 8 * g + 8)
        ys = [y[k, at, :] for k in range(3)]
        ys.append(ys[0] * ys[0] + ys[1] * ys[1] + ys[2] * ys[2] + 1.0)
        for k in range(4):
            for p, part in enumerate(thirds(ys[k])):
                pieces[3 * k + p, at, :] = part


def source_features(pieces, row):
    groups = [spread_row(pieces, k, row) for k in range(PARTS)]
    groups.append(jnp.ones((8, LANES), F32))
    groups += [jnp.zeros((8, LANES), F32)] * (LANES // 8 - len(groups))
    return jnp.concatenate(groups, axis=0).astype(BF16)


def plan_kernel(tiles, count, border_ids, sign, near, rest, sizes, selves, flags, pairs):
    clusters = selves.shape[0]
    border = border_ids.shape[0]
    tile_num = tiles.shape[1]
    dummy = clusters + 13 * border
    for c in range(clusters):
        flags[c] = 0
        pairs[c] = 0
    for b in range(border):
        flags[border_ids[b]] = 1

    middle = 13 + 9 * sign[0] + 3 * sign[1] + sign[2]
    of_ninth, of_third = 9 * (sign[0] - sign[1]), 3 * (sign[1] - sign[2])

    def place_tile(t, ends):
        recv, slot, source = tiles[0, t], tiles[1, t], tiles[2, t]
        ninth, third = (slot * 57) >> 9, (slot * 43) >> 7
        spot = middle - of_ninth * ninth - of_third * third - sign[2] * slot
        row = jnp.where(slot == 13, source, clusters + spot * border + source)
        used = (t < count[0]).astype(jnp.int32)
        seen = flags[recv]
        for which, target in enumerate((near, rest)):
            target[0, ends[which]] = recv
            target[1, ends[which]] = row
        same = jnp.logical_and(slot == 13, source == recv).astype(jnp.int32)
        pairs[recv] = pairs[recv] + used * same
        return ends[0] + used * seen, ends[1] + used * (1 - seen)

    ends = lax.fori_loop(0, tile_num, place_tile, (jnp.int32(0), jnp.int32(0)), unroll=4)
    for which, target in enumerate((near, rest)):
        for u in range(WIDE):
            target[0, ends[which] + u] = 0
            target[1, ends[which] + u] = dummy
        step = (UNROLL, WIDE)[which]
        sizes[which] = (ends[which] + step - 1) // step
    sizes[2] = (sizes[1] + 1) // 2
    for c in range(clusters):
        selves[c : c + 1, :] = jnp.full((1, LANES), pairs[c].astype(F32))


def turn_kernel(place, turned):
    eye = lax.broadcasted_iota(jnp.int32, (LANES, LANES), 0) == lax.broadcasted_iota(
        jnp.int32, (LANES, LANES), 1
    )
    eye = jnp.where(eye, 1.0, 0.0).astype(BF16)

    def turn(c, carry):
        turned[c] = lax.dot_general(
            eye, receiver_features(place, c), (((1,), (1,)), ((), ())),
            preferred_element_type=F32,
        ).astype(BF16)
        return carry

    lax.fori_loop(0, place.shape[1], turn, None, unroll=8)


def over_tiles(groups, body, step, unroll):
    def one(i, carry):
        for u in range(unroll):
            body(i * unroll + u)
        return carry

    first, end = groups if isinstance(groups, tuple) else (0, groups)
    lax.fori_loop(first * (step // unroll), end * (step // unroll), one, None)


def weigh_tiles(tiles, groups, step, turned, pieces, matrix, cubes):
    def one(t):
        recv, row = tiles[0, t], tiles[1, t]
        squared = jnp.dot(
            turned[recv], source_features(pieces, row), preferred_element_type=F32
        )
        inverse = lax.rsqrt(squared)
        second = inverse * inverse
        g3 = second * inverse
        g5 = g3 * second
        for target, value in ((matrix, g5), (cubes, g3)):
            high = value.astype(BF16)
            target[t, 0:LANES, :] = high
            target[t, LANES:, :] = (value - high.astype(F32)).astype(BF16)

    over_tiles(groups, one, step, UNROLL)


def apply_tiles(tiles, groups, step, factors, sources, matrix, sums, charges=None, cubes=None, sums_q=None):
    def one(t):
        recv, row = tiles[0, t], tiles[1, t]
        add_tile(sums, recv, WIDTH, apply(columns(factors, sources, row), matrix[t], WIDTH))
        if cubes is not None:
            left = charge_columns(factors, charges, row)
            add_tile(sums_q, recv, QWIDTH, apply(left, cubes[t], QWIDTH))

    over_tiles(groups, one, step, step)


def permanent(sums, sums_q, place, multi, selves):
    clusters = place.shape[1]
    x = [place[k] for k in range(3)]
    fields = combine(sums, x, [multi[2 + k] for k in range(6)], selves[...])
    for s in range(STATES):
        def col(c):
            return sums_q[pl.ds(s * 4 + c, clusters, stride=QWIDTH), :]

        whole = col(0)
        for b in range(3):
            fields[3 * s + b] = fields[3 * s + b] + (x[b] * whole - col(1 + b))
    return fields


class Stack:
    def __init__(self, rows):
        self.rows = rows
        self.shape = (len(rows),) + rows[0].shape

    def __getitem__(self, k):
        return self.rows[k]


def send_border(values, held, outgoing, border_ids):
    for k, value in enumerate(values):
        held[k] = value
    for b in range(outgoing.shape[1]):
        row = pl.ds(border_ids[b], 1)
        for k in range(len(values)):
            outgoing[k, pl.ds(b, 1), :] = held[k, row, :]


def first_near_kernel(where, parts_of, *refs):
    tiles, sizes, border_ids, sign, place, multi, response, turned, selves = refs[:9]
    halo = refs[9 : 9 + parts_of]
    (outgoing, matrix, factors, pieces, moments, charges, sums, sums_q,
     y, cubes, held) = refs[9 + parts_of :]
    border = outgoing.shape[1]
    reach = [BRICK * sign[a].astype(F32) for a in range(3)]
    moves = [
        [reach[a] * (1 - slot // scale % 3) for a, scale in enumerate((9, 3, 1))]
        for slot in range(27)
    ]
    own = Stack([place[k] for k in range(3)] + [multi[k] for k in range(8)])
    collect(y, 0, own, halo, where, border, moves)
    collect(charges, 3, own, halo, where, border)
    collect(moments, 5, own, halo, where, border)
    write_factors(factors, y)
    write_parts(pieces, y)
    sums[...] = jnp.zeros_like(sums)
    sums_q[...] = jnp.zeros_like(sums_q)
    weigh_tiles(tiles, sizes[0], UNROLL, turned, pieces, matrix, cubes)
    apply_tiles(tiles, sizes[0], UNROLL, factors, moments, matrix, sums, charges, cubes, sums_q)
    fields = permanent(sums, sums_q, place, multi, selves)
    send_border(
        [response[k // 3] * fields[k] for k in range(6)], held, outgoing, border_ids
    )


def first_weigh_kernel(tiles, sizes, turned, pieces, matrix, cubes):
    weigh_tiles(tiles, sizes[1], WIDE, turned, pieces, matrix, cubes)


def first_rest_kernel(tiles, sizes, place, multi, response, selves, factors,
                      moments, charges, matrix, cubes, sums_in, sums_q_in, induced, sums, sums_q):
    sums[...] = sums_in[...]
    sums_q[...] = sums_q_in[...]
    apply_tiles(tiles, sizes[1], WIDE, factors, moments, matrix, sums, charges, cubes, sums_q)
    fields = permanent(sums, sums_q, place, multi, selves)
    for k in range(6):
        induced[k] = response[k // 3] * fields[k]


def near_kernel(where, parts_of, *refs):
    tiles, sizes, border_ids, place, response, selves, factors, matrix, own = refs[:9]
    halo = refs[9 : 9 + parts_of]
    outgoing, sources, sums, held = refs[9 + parts_of :]
    collect(sources, 0, own, halo, where, outgoing.shape[1])
    sums[...] = jnp.zeros_like(sums)
    apply_tiles(tiles, sizes[0], UNROLL, factors, sources, matrix, sums)
    x = [place[k] for k in range(3)]
    fields = combine(sums, x, [own[k] for k in range(6)], selves[...])
    send_border(
        [response[k // 3] * fields[k] for k in range(6)], held, outgoing, border_ids
    )


def middle_kernel(tiles, sizes, factors, matrix, sources, sums_in, sums):
    sums[...] = sums_in[...]
    apply_tiles(tiles, sizes[2], WIDE, factors, sources, matrix, sums)


def rest_kernel(tiles, sizes, place, response, selves, factors, matrix, own, sources, sums_in,
                plain, scaled, sums):
    sums[...] = sums_in[...]
    apply_tiles(tiles, (sizes[2], sizes[1]), WIDE, factors, sources, matrix, sums)
    x = [place[k] for k in range(3)]
    fields = combine(sums, x, [own[k] for k in range(6)], selves[...])
    for k in range(6):
        plain[k] = fields[k]
        scaled[k] = response[k // 3] * fields[k]


def last_kernel(where, parts_of, border, *refs):
    near, rest, sizes, place, response, selves, factors, matrix_near, matrix_rest = refs[:9]
    plains = refs[9 : 9 + ITERS]
    scaleds = refs[9 + ITERS : 9 + 2 * ITERS]
    base = 9 + 2 * ITERS
    halo = refs[base : base + parts_of]
    gram, sources, sums = refs[base + parts_of :]
    own = scaleds[-1]
    collect(sources, 0, own, halo, where, border)
    sums[...] = jnp.zeros_like(sums)
    apply_tiles(near, sizes[0], UNROLL, factors, sources, matrix_near, sums)
    apply_tiles(rest, sizes[1], WIDE, factors, sources, matrix_rest, sums)
    x = [place[k] for k in range(3)]
    fields = combine(sums, x, [own[k] for k in range(6)], selves[...])
    lane = lax.broadcasted_iota(jnp.int32, (1, LANES), 1)
    total = jnp.zeros((1, LANES), F32)
    for s in range(STATES):
        for e, (a, b) in enumerate(GRAM):
            sum_of = None
            for k in range(3 * s, 3 * s + 3):
                right = scaleds[b][k] if b < ITERS else response[s] * fields[k]
                term = plains[a][k] * right
                sum_of = term if sum_of is None else sum_of + term
            value = jnp.sum(jnp.sum(sum_of, axis=0, keepdims=True), axis=1, keepdims=True)
            total = jnp.where(lane == s * len(GRAM) + e, value, total)
    gram[...] = jnp.broadcast_to(total, gram.shape)


def coefficients(numbers):
    def entry(a, b):
        return numbers[(a, b) if a <= b else (b, a)]

    def form(left, right, moved):
        out = None
        for a, u in enumerate(left):
            for b, w in enumerate(right):
                term = u * w * entry(a, b + moved)
                out = term if out is None else out + term
        return out

    one = jnp.ones_like(numbers[(0, 0)])
    residual, direction = [one], [one]
    weights = [jnp.zeros_like(one)] * ITERS
    norm = form(residual, residual, 0)
    for sweep in range(ITERS):
        curve = form(direction, direction, 0) - form(direction, direction, 1)
        step = norm / curve
        weights = [
            w + step * direction[k] if k < len(direction) else w for k, w in enumerate(weights)
        ]
        if sweep + 1 == ITERS:
            break
        image = direction + [jnp.zeros_like(one)]
        image = [image[0]] + [image[k] - direction[k - 1] for k in range(1, len(image))]
        residual = [
            (residual[k] if k < len(residual) else 0.0) - step * image[k] for k in range(len(image))
        ]
        after = form(residual, residual, 0)
        ratio = after / norm
        direction = [
            residual[k] + ratio * direction[k] if k < len(direction) else residual[k]
            for k in range(len(residual))
        ]
        norm = after
    return weights


def finish_kernel(grams, induced, *refs):
    scaleds = refs[:ITERS]
    inverse, result = refs[ITERS : ITERS + 2]
    total = jnp.sum(grams[...], axis=0, keepdims=True)
    rows = []
    for s in range(STATES):
        numbers = {
            pair: total[:, s * len(GRAM) + e : s * len(GRAM) + e + 1]
            for e, pair in enumerate(GRAM)
        }
        weights = coefficients(numbers)
        for k in range(3 * s, 3 * s + 3):
            value = induced[k]
            for w, scaled in zip(weights, scaleds):
                value = value + w * scaled[k]
            rows.append(value)
    done = permuted(inverse[...], rows)
    for k in range(6):
        result[k] = done[k]


def ring(cells, axis):
    count = lax.axis_size(axis)
    if count == 1:
        return [cells], (0, 0, 0)
    if count == 2:
        return [cells, lax.ppermute(cells, axis, [(0, 1), (1, 0)])], (1, 0, 1)
    steps = [1 - 2 * (i % 2) if count % 2 == 0 else 1 for i in range(count)]
    back = lax.ppermute(cells, axis, [((i - steps[i]) % count, i) for i in range(count)])
    ahead = lax.ppermute(cells, axis, [((i + steps[i]) % count, i) for i in range(count)])
    return [ahead, cells, back], (0, 1, 2)


def signs():
    which = lax.iota(jnp.int32, len(AXES))
    out = jnp.zeros_like(which)
    for a, axis in enumerate(AXES):
        count = lax.axis_size(axis)
        if count <= 2:
            sign = -1
        elif count % 2:
            sign = 1
        else:
            sign = 1 - 2 * (lax.axis_index(axis) % 2)
        out = jnp.where(which == a, sign, out)
    return out


def neighbours(cells, beside):
    first, place_x = ring(cells, "gx")
    stacked, *beside = lax.optimization_barrier((jnp.stack(first), *beside))
    second, place_y = ring(stacked, "gy")
    stacked = jnp.stack(second)
    third, place_z = ring(stacked, "gz")
    where = tuple(
        (place_z[n % 3], (place_y[n // 3 % 3], place_x[n // 9])) for n in range(27)
    )
    return third, where, beside


def shards(coords, charges, dipoles, polar, perturbed, cluster_order, border_clusters,
           tile_list, tile_count):
    atoms = coords.shape[-1]
    clusters = atoms // LANES
    border = border_clusters.shape[-1]
    tile_num = tile_list.shape[-1]
    padded = -(-(clusters + 27 * border) // LANES) * LANES

    border_ids = border_clusters.reshape(border)
    tiles = tile_list.reshape(3, tile_num)
    sign = signs()
    count = tile_count.reshape(1)
    devices = 1
    for axis in AXES:
        devices *= lax.axis_size(axis)

    cell = (clusters, LANES)
    vector = ((6,) + cell, F32)
    leave = ((6, border, LANES), F32)
    listed = -(-tile_num // WIDE) * WIDE
    matrix = ((listed, 2 * LANES, LANES), BF16)
    table = ((6, padded, LANES), F32)
    sums = ((clusters * WIDTH, LANES), F32)
    sums_q = ((clusters * QWIDTH, LANES), F32)
    listing = ((2, listed + WIDE), jnp.int32)

    whole, at = {}, 0
    for array in (coords, charges, dipoles, polar, perturbed, cluster_order, border_ids):
        array = array.reshape((1, 1, border) if array.ndim == 1 else (-1,) + cell)
        kinds = array.shape[0]
        sides = [(at, 16 - at - kinds)] + [(0, n - k) for n, k in zip(cell, array.shape[1:])]
        array = jnp.pad(array, sides)
        whole[array.dtype] = whole[array.dtype] + array if array.dtype in whole else array
        at += kinds
    whole = sum(part.astype(F32) for part in whole.values())
    place, multi, response, outgoing, order = call(
        prepare_kernel,
        [((3,) + cell, F32), ((8,) + cell, F32), ((2,) + cell, F32), ((11, border, LANES), F32),
         (cell, jnp.int32)],
        [VMEM],
    )(whole)
    near, rest, sizes, selves = call(
        plan_kernel,
        [listing, listing, ((3,), jnp.int32), (cell, F32)],
        [SMEM] * 4,
        [pltpu.SMEM((clusters,), jnp.int32)] * 2,
        outs=[SMEM] * 3 + [VMEM],
        flops=HIDDEN,
    )(tiles, count, border_ids, sign)
    (turned,) = call(
        turn_kernel, [((clusters, LANES, LANES), BF16)], [VMEM], flops=HIDDEN
    )(place)
    (inverse,) = call(inverse_kernel, [(cell, jnp.int32)], [VMEM], flops=HIDDEN)(order)

    halo, where, (turned,) = neighbours(outgoing, (turned,))
    (leaving, matrix_near, factors, pieces, moments, charge_rows, partial, partial_q) = call(
        lambda *refs: first_near_kernel(where, len(halo), *refs),
        [leave, matrix, ((padded, 4, 8, LANES), F32), ((PARTS, padded, LANES), F32), table,
         ((2, padded, LANES), F32), sums, sums_q],
        [SMEM] * 4 + [VMEM] * (5 + len(halo)),
        [pltpu.VMEM((3, padded, LANES), F32), pltpu.VMEM(*matrix), pltpu.VMEM(*vector)],
        16,
    )(near, sizes, border_ids, sign, place, multi, response, turned, selves, *halo)
    matrix_rest, cubes = call(
        first_weigh_kernel, [matrix, matrix], [SMEM] * 2 + [VMEM] * 2, flops=HIDDEN
    )(rest, sizes, turned, pieces)
    halo, where, (matrix_rest, cubes) = neighbours(leaving, (matrix_rest, cubes))
    (induced,) = call(
        first_rest_kernel, [vector], [SMEM] * 2 + [VMEM] * 11,
        [pltpu.VMEM(*sums), pltpu.VMEM(*sums_q)], flops=HIDDEN,
    )(rest, sizes, place, multi, response, selves, factors, moments, charge_rows,
      matrix_rest, cubes, partial, partial_q)

    own = induced
    plains, scaleds = [], []
    for _ in range(ITERS):
        leaving, sources, partial = call(
            lambda *refs, where=where, parts=len(halo): near_kernel(where, parts, *refs),
            [leave, table, sums], [SMEM] * 3 + [VMEM] * (6 + len(halo)),
            [pltpu.VMEM(*vector)],
        )(near, sizes, border_ids, place, response, selves, factors, matrix_near, own, *halo)
        (partial,) = call(
            middle_kernel, [sums], [SMEM] * 2 + [VMEM] * 4, flops=HIDDEN
        )(rest, sizes, factors, matrix_rest, sources, partial)
        halo, where, (partial,) = neighbours(leaving, (partial,))
        plain, own = call(
            rest_kernel, [vector, vector], [SMEM] * 2 + [VMEM] * 8, [pltpu.VMEM(*sums)],
            flops=HIDDEN,
        )(rest, sizes, place, response, selves, factors, matrix_rest, own, sources, partial)
        plains.append(plain)
        scaleds.append(own)
    (gram,) = call(
        lambda *refs: last_kernel(where, len(halo), border, *refs),
        [((devices, LANES), F32)],
        [SMEM] * 3 + [VMEM] * (6 + 2 * ITERS + len(halo)),
        [pltpu.VMEM(*table), pltpu.VMEM(*sums)],
    )(near, rest, sizes, place, response, selves, factors, matrix_near, matrix_rest,
      *plains, *scaleds, *halo)

    grams = lax.all_to_all(gram, AXES, 0, 0, tiled=True)
    (result,) = call(
        finish_kernel, [vector], [VMEM] * (3 + ITERS)
    )(grams, induced, *scaleds, inverse)
    return result.reshape(6, 1, 1, 1, atoms)


def solution(mesh):
    wide = P(None, "gx", "gy", "gz", None)
    brick = P("gx", "gy", "gz", None)
    placed = (wide, wide, wide, wide, brick, brick, brick, wide, P("gx", "gy", "gz"))
    return jax.shard_map(
        shards, mesh=mesh, in_specs=placed, out_specs=wide, check_vma=False
    )
```
